128 devices in a mesh: tx: 8 (over y, core), ty: 16 (over z, x).
Axes of the slice: x: 4, y: 4, z: 4, core: 2. Of those that a mesh axis runs over, the one named last changes fastest.
Arguments:
- increment: float32 [32, 640, 3072], P(None, 'ty', 'tx'), may hold values from -6 to 6
- vert_rate: float32 [2, 16], replicated, may hold values from 0.05 to 0.8
- zonal_rate: float32 [16, 32], replicated, may hold values from 0.003 to 0.12
- merid_rate: float32 [16, 32], replicated, may hold values from 0.02 to 0.12
- lat_band: int32 [640], replicated, may hold values from 0 to 15, never falling along the last dimension, each value on 1 to 80 neighbouring positions
- slab_owner: int32 [32], replicated, may hold values from 0 to 7, as said below
Outputs:
- covariance_product: float32 [32, 640, 3072], P(None, 'ty', 'tx')
- filtered_slabs: float32 [64, 640, 3072], P('tx', 'ty')
The draws below stay inside these ranges and needn't reach their ends.
Inputs may be any that keep to these rules, and one draw needn't show every extreme that they name: lat_band never falls along y and every band appears. `slab_owner`: each index of tx owns at most 8 slabs, and some index owns exactly 8.
All inputs are finite; a program needn't handle non-finite values.
Results may differ from the reference program's by a relative error of at most 0.0003.
Values sent between devices are 32-bit elements; how exact they have to be, the bound alone decides.
A program may use at most 128 MiB of HBM per device.

```python
import math
import jax
import jax.numpy as jnp
import numpy as np
from jax import lax

NX = 3072
NY = 640
LEV = 16
VAR = 2
NBANDS = 16
SLABS = 32
CAP = 8
N_TX = 8


def draw_slab_owner(key, part):
    groups = 2 * SLABS // CAP
    order = jax.random.permutation(jax.random.fold_in(key, 11), SLABS)
    heavy = jax.random.randint(jax.random.fold_in(key, 12), (), 0, groups)
    ranks = jnp.arange(SLABS, dtype=jnp.int32)
    others = (heavy + 1 + (ranks - CAP) % (groups - 1)) % groups
    by_rank = jnp.where(ranks < CAP, heavy, others).astype(jnp.int32)
    return jnp.zeros((SLABS,), jnp.int32).at[order].set(by_rank)


def draw_zonal_rate(key, part):
    shape = (NBANDS, SLABS)
    rates = jnp.exp(jax.random.uniform(jax.random.fold_in(key, 24), shape, jnp.float32, math.log(0.003), math.log(0.12)))
    return jnp.clip(rates, 0.003, 0.12).astype(jnp.float32)


def levels(key, dims, split, smallest, high):
    def one(dim, shards_of):
        heights = jax.random.uniform(jax.random.fold_in(jax.random.fold_in(key, 6), dim), (shards_of,), jnp.float32, smallest / len(split), high / len(split))
        return jnp.repeat(jnp.exp(heights), dims[dim] // shards_of).reshape((-1,) + (1,) * (len(dims) - dim - 1))

    gain = one(*split[0])
    for cut in split[1:]:
        gain = gain * one(*cut)
    return gain


def length_profile(amount, total, most, skew):
    weights = [(1 << 20) // math.isqrt(rank ** skew) + 1 for rank in range(2, amount + 1)]
    rest, counts = total - most - (amount - 1), [1] * (amount - 1)
    while rest > 0:
        candidates = [i for i in range(amount - 1) if counts[i] < most]
        pool, budget = sum([weights[i] for i in candidates]), rest
        for i in candidates:
            addition = min(most - counts[i], max(1, budget * weights[i] // pool), rest)
            counts[i] = counts[i] + addition
            rest = rest - addition
    return np.array([most] + counts)


def uneven(key, count, total, most, skew):
    if count == 2:
        one = jax.random.randint(key, (), max(1, total - most), min(most, total - 1) + 1)
        return jnp.stack([one, total - one])
    tallies = jnp.asarray(length_profile(count, total, most, skew), jnp.int32)
    pairs = (count - 1) // 2
    source_of, receiver = tallies[1:1 + 2 * pairs:2], tallies[2:2 + 2 * pairs:2]
    margin = jnp.minimum(source_of - 1, most - receiver)
    passed = jax.random.randint(jax.random.fold_in(key, 1), (pairs,), 0, 1 << 20) % (margin + 1)
    tallies = tallies.at[1:1 + 2 * pairs:2].set(source_of - passed).at[2:2 + 2 * pairs:2].set(receiver + passed)
    return tallies[jax.random.permutation(jax.random.fold_in(key, 2), count)]


def gaussian(key, dims, deviation, limit, shards=(), held_as=jnp.bfloat16):
    array = deviation * jax.random.normal(key, dims, jnp.float32)
    if shards:
        array = array * levels(key, dims, shards, -0.22, 0.18)
    return jnp.clip(array, -limit, limit).astype(held_as)


def setup_inputs(seed: int = 0) -> dict:
    splits = jax.random.split(jax.random.key(seed), 7)
    increment = gaussian(splits[0], (SLABS, NY, NX), 1.0, 6.0, ((1, 16), (2, 8)), jnp.float32)
    vert_rate = jnp.clip(jnp.exp(jax.random.uniform(splits[1], (VAR, LEV), jnp.float32, math.log(0.05), math.log(0.8))), 0.05, 0.8)
    zonal_rate = draw_zonal_rate(jax.random.fold_in(splits[6], 71), 0)
    merid_rate = jnp.clip(jnp.exp(jax.random.uniform(splits[3], (NBANDS, SLABS), jnp.float32, math.log(0.02), math.log(0.12))), 0.02, 0.12)
    lat_band = jnp.searchsorted(jnp.cumsum(uneven(splits[4], NBANDS, NY, 2 * NY // NBANDS, 0)), jnp.arange(NY), side="right").astype(jnp.int32)
    slab_owner = draw_slab_owner(jax.random.fold_in(splits[6], 71), 0)
    return dict(increment=increment, vert_rate=vert_rate, zonal_rate=zonal_rate, merid_rate=merid_rate, lat_band=lat_band, slab_owner=slab_owner)


def recursive_pass(values, decay, gains, reverse):
    zeros = jnp.zeros(values.shape[1:], values.dtype)
    if decay.ndim == values.ndim:

        def step(state, inputs):
            piece, dec, gain_now = inputs
            state = dec * state + gain_now * piece
            return (state, state)
        last_state, result = lax.scan(step, zeros, (values, decay, gains), reverse=reverse)
    else:

        def step_const(state, piece):
            state = decay * state + gains * piece
            return (state, state)
        last_state, result = lax.scan(step_const, zeros, values, reverse=reverse)
    return result

def smooth(values, rates):
    decay = 1.0 - rates
    gains = jnp.sqrt(rates * (2.0 - rates))
    forward = recursive_pass(values, decay, gains, False)
    return recursive_pass(forward, decay, gains, True)

def vertical_filter(values, vert_rate):
    stacked = values.reshape(VAR, LEV, NY, NX).transpose(1, 0, 2, 3)
    rates = vert_rate.T[:, :, None, None]
    result = smooth(stacked, rates)
    return result.transpose(1, 0, 2, 3).reshape(SLABS, NY, NX)

def reference(increment, vert_rate, zonal_rate, merid_rate, lat_band, slab_owner):
    vertical = vertical_filter(increment, vert_rate)
    zonal_rows = zonal_rate[lat_band].T
    zonal = smooth(vertical.transpose(2, 0, 1), zonal_rows).transpose(1, 2, 0)
    merid_rows = merid_rate[lat_band][:, :, None]
    smoothed = smooth(zonal.transpose(1, 0, 2), merid_rows).transpose(1, 0, 2)
    same = slab_owner[:, None] == slab_owner[None, :]
    earlier = jnp.arange(SLABS)[None, :] < jnp.arange(SLABS)[:, None]
    slot = lax.optimization_barrier(jnp.sum(jnp.logical_and(same, earlier), axis=1)).astype(jnp.int32)
    target = (slab_owner * CAP + slot).astype(jnp.int32)
    filtered_slabs = jnp.zeros((N_TX * CAP, NY, NX), smoothed.dtype).at[target].set(smoothed)
    covariance_product = vertical_filter(smoothed, vert_rate)
    return (covariance_product, filtered_slabs)
```

```python
import functools

import jax
import jax.numpy as jnp
from jax import lax
from jax.experimental import pallas as pl
from jax.experimental.pallas import tpu as pltpu
from jax.sharding import PartitionSpec as P

MESH = pl.DeviceIdType.MESH
F32 = jnp.float32
BF16 = jnp.bfloat16

LEV = 16
VAR = 2
NB = 16
S = 32
ROWS = 40
W = 384
COLS = 3
NT = 8
NP = 16
CAP = 8
YU = 8


def gain(rate):
    return jnp.sqrt(rate * (2.0 - rate))


def rcopy(src, dst, send, recv, dev):
    return pltpu.make_async_remote_copy(
        src_ref=src, dst_ref=dst, send_sem=send, recv_sem=recv,
        device_id=dev, device_id_type=MESH,
    )


def vertical(buf, vtab):
    def body(i, _):
        v = i // (ROWS // 8)
        rows = pl.ds(pl.multiple_of((i % (ROWS // 8)) * 8, 8), 8)
        base = v * LEV
        state = [jnp.zeros((8, 128), F32)] * COLS
        kept = []
        for l in range(LEV):
            a = vtab[0, base + l]
            g = vtab[1, base + l]
            state = [a * state[c] + g * buf[c, base + l, rows, :] for c in range(COLS)]
            kept.append(state)
        state = [jnp.zeros((8, 128), F32)] * COLS
        for l in reversed(range(LEV)):
            a = vtab[0, base + l]
            g = vtab[1, base + l]
            state = [a * state[c] + g * kept[l][c] for c in range(COLS)]
            for c in range(COLS):
                buf[c, base + l, rows, :] = state[c]
        return 0

    lax.fori_loop(0, VAR * (ROWS // 8), body, 0)


def main_kernel(
    inc, vr, zr, mr, band, owner,
    cov, recv, fbr, mt,
    vbuf, vtab, ldtab, rtab, ftab, matab, mgtab, u1, u2,
    x1h, x1l, x2h, x2l, c1s, c2s, zs, fbuf, albuf, outg, esz, ez,
    es, er, fbsend, fbrecv, fb, bb, fbs, om, otab, mtv,
    src, nxt,
    lsem, s1, r1, s2, r2, s3, r3, s4, r4, s5, r5,
):
    tx = lax.axis_index("tx")
    ty = lax.axis_index("ty")
    bar = pltpu.get_barrier_semaphore()
    for d in range(1, NT):
        pl.semaphore_signal(bar, inc=1, device_id={"tx": lax.rem(tx + d, NT)}, device_id_type=MESH)
    for d in range(1, NP):
        pl.semaphore_signal(bar, inc=1, device_id={"ty": lax.rem(ty + d, NP)}, device_id_type=MESH)
    loads = [
        pltpu.make_async_copy(inc.at[:, :, pl.ds(c * 128, 128)], vbuf.at[c], lsem.at[c])
        for c in range(COLS)
    ]
    for cp in loads:
        cp.start()

    last = [jnp.int32(S)] * NT
    for s in reversed(range(S)):
        own = owner[s]
        nx = jnp.int32(S)
        for o in range(NT):
            hit = own == o
            nx = jnp.where(hit, last[o], nx)
            last[o] = jnp.where(hit, jnp.int32(s), last[o])
        nxt[s] = nx
    nxt[S] = jnp.int32(S)
    for o in range(NT):
        cur = last[o]
        for k in range(CAP):
            src[o * CAP + k] = cur
            cur = nxt[cur]

    for v in range(VAR):
        for l in range(LEV):
            r = jnp.full((8, 128), vr[v, l], F32)
            vtab[0, v * LEV + l] = 1.0 - r
            vtab[1, v * LEV + l] = gain(r)
    eye = lax.broadcasted_iota(jnp.int32, (S, S), 0) == lax.broadcasted_iota(jnp.int32, (S, S), 1)
    lane = lax.broadcasted_iota(jnp.int32, (S, 128), 1)
    lanef = lane.astype(F32)
    sub8 = lax.broadcasted_iota(jnp.int32, (CAP, S), 0)
    slabl = lax.broadcasted_iota(jnp.int32, (CAP, S), 1)
    mine = jnp.full((CAP, S), S, jnp.int32)
    for k in range(CAP):
        mine = jnp.where(sub8 == k, src[tx * CAP + k], mine)
    sel = mine == slabl

    def table(b, _):
        zrow = jnp.broadcast_to(zr[pl.ds(b, 1), :], (S, S))
        zcol = jnp.sum(jnp.where(eye, zrow, 0.0), axis=1, keepdims=True)
        ld = jnp.broadcast_to(jnp.log1p(-zcol), (S, 128))
        ldtab[b] = ld
        for c in range(COLS):
            e = (lanef + float(c * 128)) * ld
            rtab[b, :, c * 128:(c + 1) * 128] = jnp.exp(e)
            ftab[b, :, c * 128:(c + 1) * 128] = jnp.exp(-e)
        mrow = mr[pl.ds(b, 1), :]
        mcol = jnp.sum(jnp.where(eye, jnp.broadcast_to(mrow, (S, S)), 0.0), axis=1, keepdims=True)
        mcol = jnp.broadcast_to(mcol, (S, 128))
        matab[b] = 1.0 - mcol
        mgtab[b] = gain(mcol)
        ocol = jnp.sum(jnp.where(sel, jnp.broadcast_to(mrow, (CAP, S)), 0.0), axis=1, keepdims=True)
        ocol = jnp.broadcast_to(ocol, (CAP, 128))
        otab[0, b] = 1.0 - ocol
        otab[1, b] = gain(ocol)
        return 0

    lax.fori_loop(0, NB, table, 0)

    def tri(i, _):
        rows = pl.ds(pl.multiple_of(i * 16, 16), 16)
        j = lax.broadcasted_iota(jnp.int32, (16, W + 128), 0) + i * 16
        n = lax.broadcasted_iota(jnp.int32, (16, W + 128), 1)
        u1[rows, :] = jnp.where(j <= n, 1.0, 0.0).astype(BF16)
        u2[rows, :] = jnp.where(jnp.logical_or(j > n, n >= W), 1.0, 0.0).astype(BF16)
        return 0

    lax.fori_loop(0, W // 16, tri, 0)
    for c in range(COLS):
        zs[c, S] = jnp.zeros((ROWS, 128), F32)
    fbs[S] = jnp.zeros((8, W), F32)

    for cp in loads:
        cp.wait()
    vertical(vbuf, vtab)
    vflat = vbuf.reshape(COLS, S * ROWS, 128)

    y0 = ty * ROWS

    def pass1(q, _):
        for yy in range(YU):
            y = q * YU + yy
            b = band[y0 + y]
            rows = slice(yy * S, (yy + 1) * S)
            for c in range(COLS):
                ls = slice(c * 128, (c + 1) * 128)
                u = vflat[c, pl.ds(y, S, stride=ROWS), :]
                x1 = u * ftab[b, :, ls]
                x2 = u * rtab[b, :, ls]
                h1 = x1.astype(BF16)
                h2 = x2.astype(BF16)
                x1h[rows, ls] = h1
                x2h[rows, ls] = h2
                x1l[rows, ls] = (x1 - h1.astype(F32)).astype(BF16)
                x2l[rows, ls] = (x2 - h2.astype(F32)).astype(BF16)
        rows = pl.ds(pl.multiple_of(q * (YU * S), YU * S), YU * S)
        c1s[rows, :] = jnp.dot(x1h[...], u1[...], preferred_element_type=F32) + jnp.dot(
            x1l[...], u1[...], preferred_element_type=F32)
        c2s[rows, :] = jnp.dot(x2h[...], u2[...], preferred_element_type=F32) + jnp.dot(
            x2l[...], u2[...], preferred_element_type=F32)
        return 0

    lax.fori_loop(0, ROWS // YU, pass1, 0)

    def pack(y, carry):
        e, s, ld = carry
        rows = pl.ds(pl.multiple_of(y * S, S), S)
        here = lane == y
        e = jnp.where(here, c1s[rows, W:W + 128], e)
        s = jnp.where(here, c2s[rows, W:W + 128], s)
        ld = jnp.where(here, ldtab[band[y0 + y]], ld)
        return e, s, ld

    zero = jnp.zeros((S, 128), F32)
    e, s, ld = lax.fori_loop(0, ROWS, pack, (zero, zero, zero))
    esz[0] = e * jnp.exp(float(W - 1) * ld)
    esz[1] = s
    aw = jnp.exp(float(W) * ld)
    a1 = jnp.exp(ld)

    pl.semaphore_wait(bar, NT + NP - 2)

    def x1(d, here):
        p = lax.rem(tx + d, NT)
        q = p if here else tx
        return rcopy(esz, ez.at[q], s1.at[d], r1.at[q], {"tx": p})

    for d in range(1, NT):
        x1(d, False).start()
    ez[tx] = esz[...]
    for d in range(1, NT):
        x1(d, True).wait_recv()
    rin = zero
    rmine = zero
    for t in range(NT):
        rmine = jnp.where(tx == t, rin, rmine)
        rin = ez[t, 0] + aw * rin
    tin = -a1 * rin
    tmine = zero
    for t in reversed(range(NT)):
        tmine = jnp.where(tx == t, tin, tmine)
        tin = ez[t, 1] + aw * tin
    pp = a1 * rmine
    qq = aw * tmine

    zflat = zs.reshape(COLS, (S + 1) * ROWS, 128)

    zcar = tuple(jnp.zeros((S, 128), F32) for _ in range(COLS))

    def pass2(q, carry):
        state, al = list(carry[0]), carry[1]
        for yy in range(YU):
            y = q * YU + yy
            b = band[y0 + y]
            p = jnp.sum(jnp.where(lane == y, pp, 0.0), axis=1, keepdims=True)
            qv = jnp.sum(jnp.where(lane == y, qq, 0.0), axis=1, keepdims=True)
            rows = pl.ds(pl.multiple_of(y * S, S), S)
            a = matab[b]
            g = mgtab[b]
            for c in range(COLS):
                ls = slice(c * 128, (c + 1) * 128)
                z = rtab[b, :, ls] * (c1s[rows, ls] + p) + ftab[b, :, ls] * (c2s[rows, ls] + qv)
                zflat[c, pl.ds(y, S, stride=ROWS), :] = z
                state[c] = a * state[c] + g * z
                fbuf[rows, ls] = state[c]
            al = a * al
            albuf[rows, :] = al
        return tuple(state), al

    state, al = lax.fori_loop(0, ROWS // YU, pass2, (zcar, jnp.ones((S, 128), F32)))

    def x2(d, here):
        p = lax.rem(tx + d, NT)
        q = p if here else tx
        return rcopy(outg.at[p], recv.at[q], s2.at[d], r2.at[q], {"tx": p})

    for d in (4, 5, 3, 2, 6, 7, 1, 0):
        p = lax.rem(tx + d, NT)

        def fill(k, _):
            slab = src[p * CAP + k]
            for c in range(COLS):
                outg[p, c, pl.ds(pl.multiple_of(k * ROWS, 8), ROWS), :] = zs[c, slab]
            return 0

        lax.fori_loop(0, CAP, fill, 0)
        if d:
            x2(d, False).start()
        else:
            own_copy = pltpu.make_async_copy(outg.at[tx], recv.at[tx], lsem.at[0])
            own_copy.start()

    def back(i, carry):
        st, gm = list(carry[0]), carry[1]
        for k in range(4):
            y = ROWS - 1 - (i * 4 + k)
            b = band[y0 + y]
            rows = pl.ds(pl.multiple_of(y * S, S), S)
            a = matab[b]
            g = mgtab[b]
            for c in range(COLS):
                st[c] = a * st[c] + g * fbuf[rows, c * 128:(c + 1) * 128]
            gm = a * gm + g * albuf[rows, :]
        return tuple(st), gm

    first, gm = lax.fori_loop(0, ROWS // 4, back, (zcar, zero))
    for t in range(NP):
        two = slice(2 * t, 2 * t + 2)
        for c in range(COLS):
            ls = slice(c * 128, (c + 1) * 128)
            es[t, 0:2, ls] = state[c][two]
            es[t, 2:4, ls] = first[c][two]
            es[t, 4:6, ls] = al[two]
            es[t, 6:8, ls] = gm[two]

    def x3(d, here):
        p = lax.rem(ty + d, NP)
        q = p if here else ty
        return rcopy(es.at[p], er.at[q], s3.at[d], r3.at[q], {"ty": p})

    for d in range(1, NP):
        x3(d, False).start()
    er[ty] = es[ty]
    for d in range(1, NP):
        x3(d, True).wait_recv()
    f = jnp.zeros((2, W), F32)
    for p in range(NP):
        fbsend[p, 0:2, :] = f
        f = er[p, 0:2, :] + er[p, 4:6, :] * f
    bk = jnp.zeros((2, W), F32)
    for p in reversed(range(NP)):
        fbsend[p, 2:4, :] = bk
        fbsend[p, 4:8, :] = jnp.zeros((4, W), F32)
        bk = er[p, 2:4, :] + er[p, 6:8, :] * fbsend[p, 0:2, :] + er[p, 4:6, :] * bk

    def x4(d, here):
        p = lax.rem(ty + d, NP)
        q = p if here else ty
        return rcopy(fbsend.at[p], fbrecv.at[q], s4.at[d], r4.at[q], {"ty": p})

    for d in range(1, NP):
        x4(d, False).start()
    fbrecv[ty] = fbsend[ty]
    for d in range(1, NP):
        x4(d, True).wait_recv()
    for t in range(NP):
        fb[2 * t:2 * t + 2, :] = fbrecv[t, 0:2, :]
        bb[2 * t:2 * t + 2, :] = fbrecv[t, 2:4, :]
        for j in range(2):
            fbs[2 * t + j, 0:1, :] = fbrecv[t, j:j + 1, :]
            fbs[2 * t + j, 1:2, :] = fbrecv[t, 2 + j:3 + j, :]
    for o in range(NT):
        for k in range(CAP):
            slab = src[o * CAP + k]
            om[o, 0, k:k + 1, :] = fbs[slab, 0:1, :]
            om[o, 1, k:k + 1, :] = fbs[slab, 1:2, :]

    def x5(d, here):
        p = lax.rem(tx + d, NT)
        q = p if here else tx
        return rcopy(om.at[p], fbr.at[q], s5.at[d], r5.at[q], {"tx": p})

    for d in range(1, NT):
        x5(d, False).start()
    own_fb = pltpu.make_async_copy(om.at[tx], fbr.at[tx], lsem.at[1])
    own_fb.start()

    def rates(y, _):
        b = band[y0 + y]
        mtv[0, y] = otab[0, b]
        mtv[1, y] = otab[1, b]
        return 0

    lax.fori_loop(0, ROWS, rates, 0)
    mt_copy = pltpu.make_async_copy(mtv, mt, lsem.at[2])
    mt_copy.start()

    fin = [fb[:, c * 128:(c + 1) * 128] for c in range(COLS)]

    def smooth(i, st):
        st = list(st)
        for k in range(4):
            y = ROWS - 1 - (i * 4 + k)
            b = band[y0 + y]
            rows = pl.ds(pl.multiple_of(y * S, S), S)
            a = matab[b]
            g = mgtab[b]
            alp = albuf[rows, :]
            for c in range(COLS):
                st[c] = a * st[c] + g * (fbuf[rows, c * 128:(c + 1) * 128] + alp * fin[c])
                vflat[c, pl.ds(y, S, stride=ROWS), :] = st[c]
        return tuple(st)

    lax.fori_loop(0, ROWS // 4, smooth, tuple(bb[:, c * 128:(c + 1) * 128] for c in range(COLS)))
    vertical(vbuf, vtab)
    stores = [
        pltpu.make_async_copy(vbuf.at[c], cov.at[:, :, pl.ds(c * 128, 128)], lsem.at[3 + c])
        for c in range(COLS)
    ]
    for cp in stores:
        cp.start()
    for cp in stores:
        cp.wait()
    own_copy.wait()
    own_fb.wait()
    mt_copy.wait()
    for d in range(1, NT):
        x1(d, False).wait_send()
        x2(d, False).wait_send()
        x2(d, True).wait_recv()
        x5(d, False).wait_send()
        x5(d, True).wait_recv()
    for d in range(1, NP):
        x3(d, False).wait_send()
        x4(d, False).wait_send()


def final_kernel(recv, fbr, mt, out, tmp):
    def col(c, _):
        kept = []
        f = fbr[0, 0, c]
        for y in range(ROWS):
            f = mt[0, y] * f + mt[1, y] * recv[0, c, pl.ds(y, CAP, stride=ROWS), :]
            kept.append(f)
        b = fbr[0, 1, c]
        for y in reversed(range(ROWS)):
            b = mt[0, y] * b + mt[1, y] * kept[y]
            tmp[c, pl.ds(y, CAP, stride=ROWS), :] = b
        return 0

    lax.fori_loop(0, COLS, col, 0)
    for c in range(COLS):
        for k in range(CAP):
            out[k, :, c * 128:(c + 1) * 128] = tmp[c, k * ROWS:(k + 1) * ROWS, :]


def shards(increment, vert_rate, zonal_rate, merid_rate, lat_band, slab_owner):
    vm = pltpu.VMEM
    dma = pltpu.SemaphoreType.DMA
    anyspace = pl.BlockSpec(memory_space=pl.ANY)
    vspec = pl.BlockSpec(memory_space=pltpu.VMEM)
    sspec = pl.BlockSpec(memory_space=pltpu.SMEM)
    cov, recv, fbr, mt = pl.pallas_call(
        main_kernel,
        out_shape=(
            jax.ShapeDtypeStruct((S, ROWS, W), F32),
            jax.ShapeDtypeStruct((NT, COLS, CAP * ROWS, 128), F32),
            jax.ShapeDtypeStruct((NT, 2, CAP, W), F32),
            jax.ShapeDtypeStruct((2, ROWS, CAP, 128), F32),
        ),
        in_specs=[anyspace, sspec, vspec, vspec, sspec, sspec],
        out_specs=(anyspace, anyspace, anyspace, anyspace),
        scratch_shapes=[
            vm((COLS, S, ROWS, 128), F32),
            vm((2, VAR * LEV, 8, 128), F32),
            vm((NB, S, 128), F32),
            vm((NB, S, W), F32),
            vm((NB, S, W), F32),
            vm((NB, S, 128), F32),
            vm((NB, S, 128), F32),
            vm((W, W + 128), BF16),
            vm((W, W + 128), BF16),
            vm((YU * S, W), BF16),
            vm((YU * S, W), BF16),
            vm((YU * S, W), BF16),
            vm((YU * S, W), BF16),
            vm((ROWS * S, W + 128), F32),
            vm((ROWS * S, W + 128), F32),
            vm((COLS, S + 1, ROWS, 128), F32),
            vm((ROWS * S, W), F32),
            vm((ROWS * S, 128), F32),
            vm((NT, COLS, CAP * ROWS, 128), F32),
            vm((2, S, 128), F32),
            vm((NT, 2, S, 128), F32),
            vm((NP, 8, W), F32),
            vm((NP, 8, W), F32),
            vm((NP, 8, W), F32),
            vm((NP, 8, W), F32),
            vm((S, W), F32),
            vm((S, W), F32),
            vm((S + 1, 8, W), F32),
            vm((NT, 2, CAP, W), F32),
            vm((2, NB, CAP, 128), F32),
            vm((2, ROWS, CAP, 128), F32),
            pltpu.SMEM((NT * CAP,), jnp.int32),
            pltpu.SMEM((S + 1,), jnp.int32),
            dma((6,)),
            dma((NT,)), dma((NT,)),
            dma((NT,)), dma((NT,)),
            dma((NP,)), dma((NP,)),
            dma((NP,)), dma((NP,)),
            dma((NT,)), dma((NT,)),
        ],
        compiler_params=pltpu.CompilerParams(
            collective_id=0, has_side_effects=True, vmem_limit_bytes=56 * 1024 * 1024
        ),
        name="filter_exchange",
    )(increment, vert_rate, zonal_rate, merid_rate, lat_band, slab_owner)
    fbr = fbr.reshape(NT, 2, CAP, COLS, 128).transpose(0, 1, 3, 2, 4)
    filtered = pl.pallas_call(
        final_kernel,
        grid=(NT,),
        out_shape=jax.ShapeDtypeStruct((CAP, ROWS, NT * W), F32),
        in_specs=[
            pl.BlockSpec((1, COLS, CAP * ROWS, 128), lambda t: (t, 0, 0, 0)),
            pl.BlockSpec((1, 2, COLS, CAP, 128), lambda t: (t, 0, 0, 0, 0)),
            pl.BlockSpec((2, ROWS, CAP, 128), lambda t: (0, 0, 0, 0)),
        ],
        out_specs=pl.BlockSpec((CAP, ROWS, W), lambda t: (0, 0, t)),
        scratch_shapes=[vm((COLS, CAP * ROWS, 128), F32)],
        name="owner_columns",
    )(recv, fbr, mt)
    return cov, filtered


def solution(mesh):
    return jax.shard_map(
        shards,
        mesh=mesh,
        in_specs=(P(None, "ty", "tx"), P(), P(), P(), P(), P()),
        out_specs=(P(None, "ty", "tx"), P("tx", "ty", None)),
        check_vma=False,
    )
```
